32 devices in a mesh: node: 8 (over z, y), local: 4 (over x, core).
Axes of the slice: x: 2, y: 2, z: 4, core: 2. Of those that a mesh axis runs over, the one named last changes fastest.
Arguments:
- tokens: bfloat16 [4096, 4096], P(('node', 'local')), may hold values from -6 to 6
- key_codes: bfloat16 [4096, 512], P('local'), may hold values from -0.09375 to 0.09375
- key_exponents: int32 [4096, 2], P('local'), may hold values from -1 to 1
- key_cotangent: bfloat16 [4096, 512], P(('node', 'local')), may hold values from -6 to 6
Outputs:
- keys: bfloat16 [4096, 512], P(('node', 'local'))
- input_grad: bfloat16 [4096, 4096], P(('node', 'local'))
- weight_grad: float32 [4096, 512], P(('node', 'local'))
The draws below stay inside these ranges and needn't reach their ends.
Inputs may be any that keep to these rules, and one draw needn't show every extreme that they name: key_exponents gives the power of two that scales each block of 256 columns of a row of key_codes.
All inputs are finite; a program needn't handle non-finite values.
Results may differ from the reference program's by a relative error of at most 0.015.
Values may be sent and summed in bfloat16 or wider, within the bound.
A program may use at most 128 MiB of HBM per device.

```python
import math
import jax
import jax.numpy as jnp
from jax import lax

DW = 4096
KVH = 4
HEAD = 128
QBLOCK = 256
SEQ = 8192
TOK_DEV = 128
KV = 512
TOKENS = 4096
N_NODE = 8
N_LOCAL = 4


def touch_ends(array, rng, smallest, high):
    longest = array.shape.index(max(array.shape))
    spots = []
    for shift in (0, 1):
        where = [jax.random.randint(jax.random.fold_in(rng, axis), (), 0, length) for axis, length in enumerate(array.shape)]
        where[longest] = (where[longest] + shift) % array.shape[longest]
        spots.append(tuple(where))
    return array.at[spots[0]].set(smallest).at[spots[1]].set(high)


def with_spikes(values, key, source, target, parts, factor):
    owner, partner = [(jnp.arange(values.shape[position]) // (values.shape[position] // parts)).reshape([-1 if axis == position else 1 for axis in range(values.ndim)]) for position in (source, target)]
    chosen = jax.random.permutation(key, parts)[partner]
    strong = (owner == chosen) | (owner == (partner + parts // 2) % parts)
    return jnp.where(strong, factor * values, values)


def block_levels(own_key, dims, split, least, high):
    gain = 1.0
    for axis_at, shards_of in split:
        draws = jax.random.uniform(jax.random.fold_in(jax.random.fold_in(own_key, 6), axis_at), (shards_of,), jnp.float32, least / len(split), high / len(split))
        gain = gain * jnp.repeat(jnp.exp(draws), dims[axis_at] // shards_of).reshape((-1,) + (1,) * (len(dims) - 1 - axis_at))
    return gain


def normal_values(stream_key, extent, spread, reach, cuts=(), kind=jnp.bfloat16):
    entries = spread * jax.random.normal(stream_key, extent, jnp.float32)
    if cuts:
        entries = entries * block_levels(stream_key, extent, cuts, -0.22, 0.18)
    return jnp.clip(entries, -reach, reach).astype(kind)


def bell_draw_with(stream_key, extent, deviation, limit, shards, heavy, held_as=jnp.bfloat16):
    entries = deviation * jax.random.normal(stream_key, extent, jnp.float32)
    if shards:
        entries = entries * block_levels(stream_key, extent, shards, -0.22, 0.18)
    return jnp.clip(with_spikes(entries, jax.random.fold_in(stream_key, 3), *heavy), -limit, limit).astype(held_as)


def setup_inputs(seed: int = 0) -> dict:
    streams_of = jax.random.split(jax.random.key(seed), 5)
    return {
        "tokens": bell_draw_with(streams_of[0], (TOKENS, DW), 1.0, 6.0, ((0, 32),), (0, 1, 32, 2.75)),
        "key_codes": normal_values(streams_of[1], (DW, KV), DW ** -0.5, 0.09375, ((0, 4),)),
        "key_exponents": touch_ends(jax.random.randint(streams_of[2], (DW, KV // QBLOCK), -1, 2), jax.random.fold_in(streams_of[2], 1), -1, 1).astype(jnp.int32),
        "key_cotangent": normal_values(streams_of[3], (TOKENS, KV), 1.0, 6.0, ((0, 32),)),
    }


THETA = 500000.0

def tables(positions):
    inverse = THETA ** (-(jnp.arange(HEAD // 2, dtype=jnp.float32) * 2.0 / HEAD))
    angles = positions.astype(jnp.float32)[:, None] * inverse[None, :]
    return (jnp.cos(angles), jnp.sin(angles))

def rotate(values, cosine, sine_part):
    count = values.shape[0]
    heads = values.reshape(count, KVH, HEAD)
    first_half = heads[:, :, :HEAD // 2]
    second_half = heads[:, :, HEAD // 2:]
    cos_rows = cosine[:, None, :]
    sin_rows = sine_part[:, None, :]
    joined = jnp.concatenate([first_half * cos_rows - second_half * sin_rows, second_half * cos_rows + first_half * sin_rows], axis=2)
    return joined.reshape(count, KVH * HEAD)

def unrotate(values, cosine, sine_part):
    count = values.shape[0]
    heads = values.reshape(count, KVH, HEAD)
    first_half = heads[:, :, :HEAD // 2]
    second_half = heads[:, :, HEAD // 2:]
    cos_rows = cosine[:, None, :]
    sin_rows = sine_part[:, None, :]
    joined = jnp.concatenate([first_half * cos_rows + second_half * sin_rows, second_half * cos_rows - first_half * sin_rows], axis=2)
    return joined.reshape(count, KVH * HEAD)

def quantize(partial_value):
    blocks = partial_value.reshape(partial_value.shape[0], partial_value.shape[1] // QBLOCK, QBLOCK)
    largest = lax.optimization_barrier(jnp.max(jnp.abs(blocks), axis=2))
    block_scale = jnp.exp2(jnp.ceil(jnp.log2(largest + 1e-06)))
    code_values = (blocks / block_scale[:, :, None]).astype(jnp.bfloat16)
    return (code_values, block_scale.astype(jnp.bfloat16))

def dequantize(code_values, block_scale):
    values = code_values.astype(jnp.float32) * block_scale.astype(jnp.float32)[..., None]
    return values.reshape(values.shape[0], values.shape[1] * values.shape[2])

def reference(tokens, key_codes, key_exponents, key_cotangent):
    expanded = jnp.repeat(jnp.exp2(key_exponents.astype(jnp.float32)), QBLOCK, axis=1)
    weights = (key_codes.astype(jnp.float32) * expanded).astype(jnp.bfloat16)
    positions = jnp.arange(TOKENS, dtype=jnp.int32) % SEQ
    cosine, sine_part = tables(positions)
    projected = jnp.dot(tokens, weights, preferred_element_type=jnp.float32)
    keys = rotate(projected, cosine, sine_part).astype(jnp.bfloat16)
    pre_grad = unrotate(key_cotangent.astype(jnp.float32), cosine, sine_part).astype(jnp.bfloat16)
    input_grad = lax.dot_general(pre_grad, weights, (((1,), (1,)), ((), ())), preferred_element_type=jnp.float32).astype(jnp.bfloat16)
    device_count = N_NODE * N_LOCAL

    def accumulate(summed, device_block):
        block_rows, grad_rows = device_block
        partial_value = lax.dot_general(block_rows, grad_rows, (((0,), (0,)), ((), ())), preferred_element_type=jnp.float32)
        code_values, block_scale = quantize(partial_value)
        return (summed + dequantize(code_values, block_scale), None)
    summed, _ = lax.scan(accumulate, jnp.zeros((DW, KV), jnp.float32), (tokens.reshape(device_count, TOK_DEV, DW), pre_grad.reshape(device_count, TOK_DEV, KV)))
    weight_grad = summed * (1.0 / math.sqrt(TOKENS))
    return (keys, input_grad, weight_grad)
```

```python
import functools
import math

import jax
import jax.numpy as jnp
import numpy as np
from jax import lax
from jax.experimental import pallas as pl
from jax.experimental.pallas import tpu as pltpu
from jax.sharding import PartitionSpec as P

KVH = 4
HEAD = 128
QBLOCK = 256
SEQ = 8192
MESH = pl.DeviceIdType.MESH


THETA = 500000.0


def tables(positions):
    inverse = THETA ** (-(jnp.arange(HEAD // 2, dtype=jnp.float32) * 2.0 / HEAD))
    angles = positions.astype(jnp.float32)[:, None] * inverse[None, :]
    return (jnp.cos(angles), jnp.sin(angles))


def rotate(values, cosine, sine_part):
    count = values.shape[0]
    heads = values.reshape(count, KVH, HEAD)
    first_half = heads[:, :, : HEAD // 2]
    second_half = heads[:, :, HEAD // 2 :]
    cos_rows = cosine[:, None, :]
    sin_rows = sine_part[:, None, :]
    joined = jnp.concatenate(
        [
            first_half * cos_rows - second_half * sin_rows,
            second_half * cos_rows + first_half * sin_rows,
        ],
        axis=2,
    )
    return joined.reshape(count, KVH * HEAD)


def unrotate(values, cosine, sine_part):
    count = values.shape[0]
    heads = values.reshape(count, KVH, HEAD)
    first_half = heads[:, :, : HEAD // 2]
    second_half = heads[:, :, HEAD // 2 :]
    cos_rows = cosine[:, None, :]
    sin_rows = sine_part[:, None, :]
    joined = jnp.concatenate(
        [
            first_half * cos_rows + second_half * sin_rows,
            second_half * cos_rows - first_half * sin_rows,
        ],
        axis=2,
    )
    return joined.reshape(count, KVH * HEAD)


def quantize(partial_value):
    blocks = partial_value.reshape(partial_value.shape[0], partial_value.shape[1] // QBLOCK, QBLOCK)
    largest = jnp.max(jnp.abs(blocks), axis=2)
    block_scale = jnp.exp2(jnp.ceil(jnp.log2(largest + 1e-06)))
    code_values = (blocks / block_scale[:, :, None]).astype(jnp.bfloat16)
    return (code_values, block_scale.astype(jnp.bfloat16))


def expand_codes(code_values, block_scale):
    lead = code_values.shape[:-1]
    blocks = code_values.reshape(lead + (block_scale.shape[-1], QBLOCK))
    values = blocks.astype(jnp.float32) * block_scale.astype(jnp.float32)[..., None]
    return values.reshape(lead + (code_values.shape[-1],))


def on_device(tokens, key_codes, key_exponents, key_cotangent):
    node_count = lax.axis_size("node")
    local_count = lax.axis_size("local")
    tok_count = tokens.shape[0]
    width = tokens.shape[1]
    feature_count = key_codes.shape[1]
    expanded = jnp.repeat(jnp.exp2(key_exponents.astype(jnp.float32)), QBLOCK, axis=1)
    shard_weights = (key_codes.astype(jnp.float32) * expanded).astype(jnp.bfloat16)
    weights = lax.all_gather(shard_weights, "local", axis=0, tiled=True)
    device_index = lax.axis_index("node") * local_count + lax.axis_index("local")
    positions = (device_index * tok_count + jnp.arange(tok_count, dtype=jnp.int32)) % SEQ
    cosine, sine_part = tables(positions)
    pre_grad = unrotate(key_cotangent.astype(jnp.float32), cosine, sine_part).astype(jnp.bfloat16)
    partial_value = lax.dot_general(
        tokens, pre_grad, (((0,), (0,)), ((), ())), preferred_element_type=jnp.float32
    )
    code_values, block_scale = quantize(partial_value)
    row_count = width // (node_count * local_count)
    block_count = feature_count // QBLOCK
    code_grid = code_values.reshape(node_count, local_count, row_count, feature_count)
    scale_grid = block_scale.reshape(node_count, local_count, row_count, block_count)
    projected = jnp.dot(tokens, weights, preferred_element_type=jnp.float32)
    keys = rotate(projected, cosine, sine_part).astype(jnp.bfloat16)
    input_grad = lax.dot_general(
        pre_grad, weights, (((1,), (1,)), ((), ())), preferred_element_type=jnp.float32
    ).astype(jnp.bfloat16)
    got_codes, got_scales = (
        lax.all_to_all(code_grid, "local", split_axis=1, concat_axis=1, tiled=True),
        lax.all_to_all(scale_grid, "local", split_axis=1, concat_axis=1, tiled=True),
    )
    node_terms = jnp.sum(expand_codes(got_codes, got_scales), axis=1)
    summed = (
        lax.psum_scatter(node_terms.astype(jnp.bfloat16), "node", scatter_dimension=0, tiled=True)
        .astype(jnp.float32)
        .reshape(row_count, feature_count)
    )
    total_tokens = tok_count * node_count * local_count
    weight_grad = summed * (1.0 / math.sqrt(total_tokens))
    return (keys, input_grad, weight_grad)


def flip(index, distance):
    result = index
    bit = 1
    while bit <= distance:
        if distance & bit:
            result = result + bit - 2 * bit * lax.rem(lax.div(index, bit), 2)
        bit *= 2
    return result


def turn(values, cosine, signed_sine):
    parts = []
    for head in range(values.shape[1] // HEAD):
        piece = values[:, head * HEAD : (head + 1) * HEAD]
        parts.append(piece * cosine + pltpu.roll(piece, HEAD // 2, 1) * signed_sine)
    return jnp.concatenate(parts, axis=1)


def fused_kernel(
    nodes,
    locals_,
    chunks,
    tokens_hbm,
    codes_hbm,
    exponents_ref,
    cotangent_ref,
    inverse_ref,
    keys_ref,
    input_grad_ref,
    weight_grad_ref,
    tokens,
    codes,
    columns,
    pre,
    weights,
    outgoing,
    incoming,
    load_sem,
    own_sem,
    column_send,
    column_recv,
    pre_send,
    pre_recv,
    peer_send,
    core_send,
    weight_recv,
    sum_send,
    sum_recv,
):
    node = lax.axis_index("node")
    local = lax.axis_index("local")
    count = tokens.shape[0]
    row_count = columns.shape[2]
    shard_rows = weights.shape[1]
    chunk_rows = shard_rows // chunks
    total = count * nodes * locals_

    barrier = pltpu.get_barrier_semaphore()
    for d in range(1, locals_):
        pl.semaphore_signal(barrier, inc=1, device_id=(node, flip(local, d)), device_id_type=MESH)
    for e in range(1, nodes):
        pl.semaphore_signal(barrier, inc=1, device_id=(flip(node, e), local), device_id_type=MESH)

    load_codes = pltpu.make_async_copy(codes_hbm, codes, load_sem.at[0])
    load_codes.start()
    load_tokens = pltpu.make_async_copy(tokens_hbm, tokens, load_sem.at[1])
    load_tokens.start()

    def owned(e, d):
        first = (flip(node, e) * locals_ + flip(local, d)) * row_count
        return pl.ds(pl.multiple_of(first, row_count), row_count)

    order = list(range(nodes - 1, -1, -1))
    own = {}
    for e in order:
        own[e] = pltpu.make_async_copy(
            tokens_hbm.at[:, owned(e, 0)], columns.at[e, pl.ds(0, count), :], own_sem.at[e]
        )
        own[e].start()

    start = lax.rem((node * locals_ + local) * count, SEQ)
    positions = lax.rem(start + lax.broadcasted_iota(jnp.int32, (count, HEAD), 0), SEQ)
    angles = positions.astype(jnp.float32) * inverse_ref[...]
    cosine = jnp.cos(angles)
    sine = jnp.sin(angles)
    lane = lax.broadcasted_iota(jnp.int32, (count, HEAD), 1)
    signed_sine = jnp.where(lane < HEAD // 2, -sine, sine)
    pre[pl.ds(0, count), :] = turn(
        cotangent_ref[...].astype(jnp.float32), cosine, -signed_sine
    ).astype(jnp.bfloat16)

    pl.semaphore_wait(barrier, locals_ - 1 + nodes - 1)

    sends = []
    pre_copies = {}
    for d in range(1, locals_):
        pre_copies[d] = pltpu.make_async_remote_copy(
            src_ref=pre.at[pl.ds(0, count), :],
            dst_ref=pre.at[pl.ds(d * count, count), :],
            send_sem=pre_send.at[d],
            recv_sem=pre_recv.at[d],
            device_id=(node, flip(local, d)),
            device_id_type=MESH,
        )
        pre_copies[d].start()
        sends.append(pre_copies[d])
    column_copies = {}
    for e in order:
        for d in range(locals_ - 1, 0, -1):
            copy = pltpu.make_async_remote_copy(
                src_ref=tokens_hbm.at[:, owned(e, d)],
                dst_ref=columns.at[e, pl.ds(d * count, count), :],
                send_sem=column_send.at[e, d],
                recv_sem=column_recv.at[e, d],
                device_id=(node, flip(local, d)),
                device_id_type=MESH,
            )
            copy.start()
            column_copies[e, d] = copy
            sends.append(copy)

    def weight_copy(source, slot, part, distance, send_sem):
        rows = pl.ds(part * chunk_rows, chunk_rows)
        return pltpu.make_async_remote_copy(
            src_ref=weights.at[source, rows, :],
            dst_ref=weights.at[slot, rows, :],
            send_sem=send_sem,
            recv_sem=weight_recv.at[slot, part],
            device_id=(node, flip(local, distance)),
            device_id_type=MESH,
        )

    load_codes.wait()
    weight_copies = {}
    for part in range(chunks):
        rows = pl.ds(part * chunk_rows, chunk_rows)
        scale = jnp.left_shift(1, exponents_ref[rows, :] + 15).astype(jnp.float32) * (2.0**-15)
        for block in range(codes.shape[1] // QBLOCK):
            lanes = pl.ds(block * QBLOCK, QBLOCK)
            weights[0, rows, lanes] = (
                codes[rows, lanes].astype(jnp.float32) * scale[:, block : block + 1]
            ).astype(jnp.bfloat16)
        for d in range(2, locals_, 2):
            copy = weight_copy(0, d, part, d, peer_send.at[d // 2, part])
            copy.start()
            weight_copies[d, part] = copy
            sends.append(copy)
        copy = weight_copy(0, 1, part, 1, core_send.at[0, part])
        copy.start()
        weight_copies[1, part] = copy
        sends.append(copy)

    for d in range(1, locals_):
        pre_copies[d].wait_recv()
    summed = None
    sum_copies = {}
    for e in order:
        own[e].wait()
        for d in range(1, locals_):
            column_copies[e, d].wait_recv()
        piece = lax.dot_general(
            columns[e], pre[...], (((0,), (0,)), ((), ())), preferred_element_type=jnp.float32
        )
        if e == 0:
            summed = piece
        else:
            outgoing[e] = piece.astype(jnp.bfloat16)
            copy = pltpu.make_async_remote_copy(
                src_ref=outgoing.at[e],
                dst_ref=incoming.at[e],
                send_sem=sum_send.at[e],
                recv_sem=sum_recv.at[e],
                device_id=(flip(node, e), local),
                device_id_type=MESH,
            )
            copy.start()
            sum_copies[e] = copy
            sends.append(copy)

    load_tokens.wait()
    projected = jnp.zeros((count, weights.shape[2]), jnp.float32)

    def use(slot, part, projected):
        rows = pl.ds(part * chunk_rows, chunk_rows)
        first = flip(local, slot) * shard_rows + part * chunk_rows
        lanes = pl.ds(pl.multiple_of(first, chunk_rows), chunk_rows)
        block = weights[slot, rows, :]
        input_grad_ref[:, lanes] = lax.dot_general(
            pre[pl.ds(0, count), :],
            block,
            (((1,), (1,)), ((), ())),
            preferred_element_type=jnp.float32,
        ).astype(jnp.bfloat16)
        return projected + jnp.dot(tokens[:, lanes], block, preferred_element_type=jnp.float32)

    for part in range(chunks):
        projected = use(0, part, projected)
    for part in range(chunks):
        weight_copies[1, part].wait_recv()
        projected = use(1, part, projected)
    for part in range(chunks):
        for d in range(2, locals_, 2):
            weight_copies[d, part].wait_recv()
            copy = weight_copy(d, d + 1, part, 1, core_send.at[d // 2, part])
            copy.start()
            weight_copies[d + 1, part] = copy
            sends.append(copy)
            projected = use(d, part, projected)
        for d in range(2, locals_, 2):
            weight_copies[d + 1, part].wait_recv()
            projected = use(d + 1, part, projected)
    keys_ref[...] = turn(projected, cosine, signed_sine).astype(jnp.bfloat16)

    for e in order[:-1]:
        sum_copies[e].wait_recv()
        summed = summed + incoming[e].astype(jnp.float32)
    weight_grad_ref[...] = summed * (1.0 / math.sqrt(total))
    for copy in sends:
        copy.wait_send()


def fused(tokens, key_codes, key_exponents, key_cotangent):
    nodes = lax.axis_size("node")
    locals_ = lax.axis_size("local")
    count, width = tokens.shape
    features = key_codes.shape[1]
    shard_rows = key_codes.shape[0]
    row_count = width // (nodes * locals_)
    chunks = 4
    half = THETA ** (-(np.arange(HEAD // 2) * 2.0 / HEAD))
    inverse = jnp.asarray(np.concatenate([half, half])[None, :], jnp.float32)
    anywhere = pl.BlockSpec(memory_space=pl.ANY)
    vmem = pl.BlockSpec(memory_space=pltpu.VMEM)
    dma = pltpu.SemaphoreType.DMA
    pairs = locals_ // 2
    return pl.pallas_call(
        functools.partial(fused_kernel, nodes, locals_, chunks),
        out_shape=(
            jax.ShapeDtypeStruct((count, features), jnp.bfloat16),
            jax.ShapeDtypeStruct((count, width), jnp.bfloat16),
            jax.ShapeDtypeStruct((row_count, features), jnp.float32),
        ),
        in_specs=[anywhere, anywhere, vmem, vmem, vmem],
        out_specs=(vmem, vmem, vmem),
        scratch_shapes=[
            pltpu.VMEM((count, width), jnp.bfloat16),
            pltpu.VMEM((shard_rows, features), jnp.bfloat16),
            pltpu.VMEM((nodes, locals_ * count, row_count), jnp.bfloat16),
            pltpu.VMEM((locals_ * count, features), jnp.bfloat16),
            pltpu.VMEM((locals_, shard_rows, features), jnp.bfloat16),
            pltpu.VMEM((nodes, row_count, features), jnp.bfloat16),
            pltpu.VMEM((nodes, row_count, features), jnp.bfloat16),
            dma((2,)),
            dma((nodes,)),
            dma((nodes, locals_)),
            dma((nodes, locals_)),
            dma((locals_,)),
            dma((locals_,)),
            dma((pairs, chunks)),
            dma((pairs, chunks)),
            dma((locals_, chunks)),
            dma((nodes,)),
            dma((nodes,)),
        ],
        compiler_params=pltpu.CompilerParams(collective_id=0, has_side_effects=True),
    )(tokens, key_codes, key_exponents, key_cotangent, inverse)


def solution(mesh):
    def body(tokens, key_codes, key_exponents, key_cotangent):
        row_count = tokens.shape[1] // (mesh.shape["node"] * mesh.shape["local"])
        run = fused if row_count % HEAD == 0 else on_device
        return run(tokens, key_codes, key_exponents, key_cotangent)

    return jax.shard_map(
        body,
        mesh=mesh,
        in_specs=(
            P(("node", "local"), None),
            P("local", None),
            P("local", None),
            P(("node", "local"), None),
        ),
        out_specs=(
            P(("node", "local"), None),
            P(("node", "local"), None),
            P(("node", "local"), None),
        ),
        check_vma=False,
    )
```

```python
import functools
import math

import jax
import jax.numpy as jnp
import numpy as np
from jax import lax
from jax.experimental import pallas as pl
from jax.experimental.pallas import tpu as pltpu
from jax.sharding import PartitionSpec as P

KVH = 4
HEAD = 128
QBLOCK = 256
SEQ = 8192
MESH = pl.DeviceIdType.MESH


THETA = 500000.0


def tables(positions):
    inverse = THETA ** (-(jnp.arange(HEAD // 2, dtype=jnp.float32) * 2.0 / HEAD))
    angles = positions.astype(jnp.float32)[:, None] * inverse[None, :]
    return (jnp.cos(angles), jnp.sin(angles))


def rotate(values, cosine, sine_part):
    count = values.shape[0]
    heads = values.reshape(count, KVH, HEAD)
    first_half = heads[:, :, : HEAD // 2]
    second_half = heads[:, :, HEAD // 2 :]
    cos_rows = cosine[:, None, :]
    sin_rows = sine_part[:, None, :]
    joined = jnp.concatenate(
        [
            first_half * cos_rows - second_half * sin_rows,
            second_half * cos_rows + first_half * sin_rows,
        ],
        axis=2,
    )
    return joined.reshape(count, KVH * HEAD)


def unrotate(values, cosine, sine_part):
    count = values.shape[0]
    heads = values.reshape(count, KVH, HEAD)
    first_half = heads[:, :, : HEAD // 2]
    second_half = heads[:, :, HEAD // 2 :]
    cos_rows = cosine[:, None, :]
    sin_rows = sine_part[:, None, :]
    joined = jnp.concatenate(
        [
            first_half * cos_rows + second_half * sin_rows,
            second_half * cos_rows - first_half * sin_rows,
        ],
        axis=2,
    )
    return joined.reshape(count, KVH * HEAD)


def quantize(partial_value):
    blocks = partial_value.reshape(partial_value.shape[0], partial_value.shape[1] // QBLOCK, QBLOCK)
    largest = jnp.max(jnp.abs(blocks), axis=2)
    block_scale = jnp.exp2(jnp.ceil(jnp.log2(largest + 1e-06)))
    code_values = (blocks / block_scale[:, :, None]).astype(jnp.bfloat16)
    return (code_values, block_scale.astype(jnp.bfloat16))


def expand_codes(code_values, block_scale):
    lead = code_values.shape[:-1]
    blocks = code_values.reshape(lead + (block_scale.shape[-1], QBLOCK))
    values = blocks.astype(jnp.float32) * block_scale.astype(jnp.float32)[..., None]
    return values.reshape(lead + (code_values.shape[-1],))


def on_device(tokens, key_codes, key_exponents, key_cotangent):
    node_count = lax.axis_size("node")
    local_count = lax.axis_size("local")
    tok_count = tokens.shape[0]
    width = tokens.shape[1]
    feature_count = key_codes.shape[1]
    expanded = jnp.repeat(jnp.exp2(key_exponents.astype(jnp.float32)), QBLOCK, axis=1)
    shard_weights = (key_codes.astype(jnp.float32) * expanded).astype(jnp.bfloat16)
    weights = lax.all_gather(shard_weights, "local", axis=0, tiled=True)
    device_index = lax.axis_index("node") * local_count + lax.axis_index("local")
    positions = (device_index * tok_count + jnp.arange(tok_count, dtype=jnp.int32)) % SEQ
    cosine, sine_part = tables(positions)
    pre_grad = unrotate(key_cotangent.astype(jnp.float32), cosine, sine_part).astype(jnp.bfloat16)
    partial_value = lax.dot_general(
        tokens, pre_grad, (((0,), (0,)), ((), ())), preferred_element_type=jnp.float32
    )
    code_values, block_scale = quantize(partial_value)
    row_count = width // (node_count * local_count)
    block_count = feature_count // QBLOCK
    code_grid = code_values.reshape(node_count, local_count, row_count, feature_count)
    scale_grid = block_scale.reshape(node_count, local_count, row_count, block_count)
    projected = jnp.dot(tokens, weights, preferred_element_type=jnp.float32)
    keys = rotate(projected, cosine, sine_part).astype(jnp.bfloat16)
    input_grad = lax.dot_general(
        pre_grad, weights, (((1,), (1,)), ((), ())), preferred_element_type=jnp.float32
    ).astype(jnp.bfloat16)
    got_codes, got_scales = (
        lax.all_to_all(code_grid, "local", split_axis=1, concat_axis=1, tiled=True),
        lax.all_to_all(scale_grid, "local", split_axis=1, concat_axis=1, tiled=True),
    )
    node_terms = jnp.sum(expand_codes(got_codes, got_scales), axis=1)
    summed = (
        lax.psum_scatter(node_terms.astype(jnp.bfloat16), "node", scatter_dimension=0, tiled=True)
        .astype(jnp.float32)
        .reshape(row_count, feature_count)
    )
    total_tokens = tok_count * node_count * local_count
    weight_grad = summed * (1.0 / math.sqrt(total_tokens))
    return (keys, input_grad, weight_grad)


def flip(index, distance):
    result = index
    bit = 1
    while bit <= distance:
        if distance & bit:
            result = result + bit - 2 * bit * lax.rem(lax.div(index, bit), 2)
        bit *= 2
    return result


def turn(values, cosine, signed_sine):
    parts = []
    for head in range(values.shape[1] // HEAD):
        piece = values[:, head * HEAD : (head + 1) * HEAD]
        parts.append(piece * cosine + pltpu.roll(piece, HEAD // 2, 1) * signed_sine)
    return jnp.concatenate(parts, axis=1)


def fused_kernel(
    nodes,
    locals_,
    chunks,
    tokens_hbm,
    codes_hbm,
    exponents_ref,
    cotangent_ref,
    inverse_ref,
    keys_ref,
    input_grad_ref,
    weight_grad_ref,
    tokens,
    codes,
    columns,
    pre,
    weights,
    outgoing,
    incoming,
    load_sem,
    own_sem,
    column_send,
    column_recv,
    pre_send,
    pre_recv,
    weight_send,
    across_send,
    weight_recv,
    sum_send,
    sum_recv,
):
    node = lax.axis_index("node")
    local = lax.axis_index("local")
    count = tokens.shape[0]
    row_count = columns.shape[2]
    shard_rows = weights.shape[1]
    chunk_rows = shard_rows // chunks
    total = count * nodes * locals_

    barrier = pltpu.get_barrier_semaphore()
    for d in range(1, locals_):
        pl.semaphore_signal(barrier, inc=1, device_id=(node, flip(local, d)), device_id_type=MESH)
    for e in range(1, nodes):
        pl.semaphore_signal(barrier, inc=1, device_id=(flip(node, e), local), device_id_type=MESH)

    load_codes = pltpu.make_async_copy(codes_hbm, codes, load_sem.at[0])
    load_codes.start()
    load_tokens = pltpu.make_async_copy(tokens_hbm, tokens, load_sem.at[1])
    load_tokens.start()

    def owned(e, d):
        first = (flip(node, e) * locals_ + flip(local, d)) * row_count
        return pl.ds(pl.multiple_of(first, row_count), row_count)

    order = list(range(nodes - 1, -1, -1))
    own = {}
    for e in order:
        own[e] = pltpu.make_async_copy(
            tokens_hbm.at[:, owned(e, 0)], columns.at[e, pl.ds(0, count), :], own_sem.at[e]
        )
        own[e].start()

    start = lax.rem((node * locals_ + local) * count, SEQ)
    positions = lax.rem(start + lax.broadcasted_iota(jnp.int32, (count, HEAD), 0), SEQ)
    angles = positions.astype(jnp.float32) * inverse_ref[...]
    cosine = jnp.cos(angles)
    sine = jnp.sin(angles)
    lane = lax.broadcasted_iota(jnp.int32, (count, HEAD), 1)
    signed_sine = jnp.where(lane < HEAD // 2, -sine, sine)
    pre[pl.ds(0, count), :] = turn(
        cotangent_ref[...].astype(jnp.float32), cosine, -signed_sine
    ).astype(jnp.bfloat16)

    pl.semaphore_wait(barrier, locals_ - 1 + nodes - 1)

    sends = []

    def send_pre(source, slot, distance):
        copy = pltpu.make_async_remote_copy(
            src_ref=pre.at[pl.ds(source * count, count), :],
            dst_ref=pre.at[pl.ds(slot * count, count), :],
            send_sem=pre_send.at[slot],
            recv_sem=pre_recv.at[slot],
            device_id=(node, flip(local, distance)),
            device_id_type=MESH,
        )
        copy.start()
        sends.append(copy)
        return copy

    pre_copies = {d: send_pre(0, d, d) for d in range(2, locals_, 2)}
    pre_copies[1] = send_pre(0, 1, 1)
    column_copies = {}
    for e in order:
        for d in range(locals_ - 1, 0, -1):
            copy = pltpu.make_async_remote_copy(
                src_ref=tokens_hbm.at[:, owned(e, d)],
                dst_ref=columns.at[e, pl.ds(d * count, count), :],
                send_sem=column_send.at[e, d],
                recv_sem=column_recv.at[e, d],
                device_id=(node, flip(local, d)),
                device_id_type=MESH,
            )
            copy.start()
            column_copies[e, d] = copy
            sends.append(copy)

    half = lax.rem(node, 2)

    def rows_of(turn_at, via):
        part = turn_at * 2 + (1 - half if via else half)
        return pl.ds(pl.multiple_of(part * chunk_rows, chunk_rows), chunk_rows)

    def send_weights(source, slot, turn_at, via, device, kind, landing):
        copy = pltpu.make_async_remote_copy(
            src_ref=weights.at[source, rows_of(turn_at, via), :],
            dst_ref=weights.at[slot, rows_of(turn_at, via), :],
            send_sem=kind.at[slot, turn_at, via],
            recv_sem=weight_recv.at[slot, turn_at, landing],
            device_id=device,
            device_id_type=MESH,
        )
        copy.start()
        sends.append(copy)
        return copy

    partner = (node, flip(local, 1))
    across = (flip(node, 1), local)
    turns = chunks // 2
    load_codes.wait()
    scale = jnp.left_shift(1, exponents_ref[...] + 15).astype(jnp.float32) * (2.0**-15)
    scale = jnp.transpose(jnp.concatenate([scale] * (8 // scale.shape[0]), axis=0))
    for block in range(codes.shape[1] // QBLOCK):
        lanes = pl.ds(block * QBLOCK, QBLOCK)
        weights[0, :, lanes] = (
            codes[:, lanes].astype(jnp.float32) * scale[:, block : block + 1]
        ).astype(jnp.bfloat16)
    arrivals = {}
    for turn_at in range(turns):
        for d in range(2, locals_, 2):
            device = (node, flip(local, d))
            arrivals[d, turn_at, 0] = send_weights(0, d, turn_at, 0, device, weight_send, 0)
        for via in range(2):
            arrivals[1, turn_at, via] = send_weights(0, 1, turn_at, via, partner, weight_send, via)

    for d in range(2, locals_, 2):
        pre_copies[d].wait_recv()
        pre_copies[d + 1] = send_pre(d, d + 1, 1)
    pre_copies[1].wait_recv()
    for d in range(3, locals_, 2):
        pre_copies[d].wait_recv()
    load_tokens.wait()
    projected = jnp.zeros((count, weights.shape[2]), jnp.float32)

    def use(slot, turn_at, via, projected):
        rows = rows_of(turn_at, via)
        first = flip(local, slot) * shard_rows + rows.start
        lanes = pl.ds(pl.multiple_of(first, chunk_rows), chunk_rows)
        block = weights[slot, rows, :]
        input_grad_ref[:, lanes] = lax.dot_general(
            pre[pl.ds(0, count), :],
            block,
            (((1,), (1,)), ((), ())),
            preferred_element_type=jnp.float32,
        ).astype(jnp.bfloat16)
        return projected + jnp.dot(tokens[:, lanes], block, preferred_element_type=jnp.float32)

    def late(turn_at, projected):
        for d in range(2, locals_, 2):
            arrivals[d, turn_at, 1].wait_recv()
            arrivals[d + 1, turn_at, 1] = send_weights(
                d, d + 1, turn_at, 1, partner, weight_send, 1
            )
            projected = use(d, turn_at, 1, projected)
        for d in range(3, locals_, 2):
            arrivals[d, turn_at, 1].wait_recv()
            projected = use(d, turn_at, 1, projected)
        return projected

    early = [(0, t, v) for t in range(turns) for v in range(2)]
    early += [(1, t, v) for t in range(turns) for v in range(2)]
    summed = None
    sum_copies = {}
    for e in order:
        own[e].wait()
        for d in range(1, locals_):
            column_copies[e, d].wait_recv()
        piece = lax.dot_general(
            columns[e], pre[...], (((0,), (0,)), ((), ())), preferred_element_type=jnp.float32
        )
        if e == 0:
            summed = piece
        else:
            outgoing[e] = piece.astype(jnp.bfloat16)
            copy = pltpu.make_async_remote_copy(
                src_ref=outgoing.at[e],
                dst_ref=incoming.at[e],
                send_sem=sum_send.at[e],
                recv_sem=sum_recv.at[e],
                device_id=(flip(node, e), local),
                device_id_type=MESH,
            )
            copy.start()
            sum_copies[e] = copy
            sends.append(copy)
        for _ in range(min(2, len(early))):
            slot, turn_at, via = early.pop(0)
            if slot == 1:
                arrivals[1, turn_at, via].wait_recv()
            projected = use(slot, turn_at, via, projected)

    for slot, turn_at, via in early:
        if slot == 1:
            arrivals[1, turn_at, via].wait_recv()
        projected = use(slot, turn_at, via, projected)
    for turn_at in range(turns):
        for d in range(2, locals_, 2):
            arrivals[d, turn_at, 0].wait_recv()
            arrivals[d, turn_at, 1] = send_weights(
                d, d, turn_at, 0, across, across_send, 1
            )
            arrivals[d + 1, turn_at, 0] = send_weights(
                d, d + 1, turn_at, 0, partner, weight_send, 0
            )
            projected = use(d, turn_at, 0, projected)
        for d in range(3, locals_, 2):
            arrivals[d, turn_at, 0].wait_recv()
            projected = use(d, turn_at, 0, projected)
        if turn_at > 0:
            projected = late(turn_at - 1, projected)
    projected = late(turns - 1, projected)
    keys_ref[...] = turn(projected, cosine, signed_sine).astype(jnp.bfloat16)

    for e in order[:-1]:
        sum_copies[e].wait_recv()
        summed = summed + incoming[e].astype(jnp.float32)
    weight_grad_ref[...] = summed * (1.0 / math.sqrt(total))
    for copy in sends:
        copy.wait_send()


def fused(tokens, key_codes, key_exponents, key_cotangent):
    nodes = lax.axis_size("node")
    locals_ = lax.axis_size("local")
    count, width = tokens.shape
    features = key_codes.shape[1]
    shard_rows = key_codes.shape[0]
    row_count = width // (nodes * locals_)
    chunks = 8
    half = THETA ** (-(np.arange(HEAD // 2) * 2.0 / HEAD))
    inverse = jnp.asarray(np.concatenate([half, half])[None, :], jnp.float32)
    anywhere = pl.BlockSpec(memory_space=pl.ANY)
    vmem = pl.BlockSpec(memory_space=pltpu.VMEM)
    dma = pltpu.SemaphoreType.DMA
    return pl.pallas_call(
        functools.partial(fused_kernel, nodes, locals_, chunks),
        out_shape=(
            pltpu.VMEM((count, features), jnp.bfloat16),
            pltpu.VMEM((count, width), jnp.bfloat16),
            pltpu.VMEM((row_count, features), jnp.float32),
        ),
        in_specs=[anywhere, anywhere, vmem, vmem, vmem],
        out_specs=(vmem, vmem, vmem),
        scratch_shapes=[
            pltpu.VMEM((count, width), jnp.bfloat16),
            pltpu.VMEM((shard_rows, features), jnp.bfloat16),
            pltpu.VMEM((nodes, locals_ * count, row_count), jnp.bfloat16),
            pltpu.VMEM((locals_ * count, features), jnp.bfloat16),
            pltpu.VMEM((locals_, shard_rows, features), jnp.bfloat16),
            pltpu.VMEM((nodes, row_count, features), jnp.bfloat16),
            pltpu.VMEM((nodes, row_count, features), jnp.bfloat16),
            dma((2,)),
            dma((nodes,)),
            dma((nodes, locals_)),
            dma((nodes, locals_)),
            dma((locals_,)),
            dma((locals_,)),
            dma((locals_, chunks // 2, 2)),
            dma((locals_, chunks // 2, 2)),
            dma((locals_, chunks // 2, 2)),
            dma((nodes,)),
            dma((nodes,)),
        ],
        compiler_params=pltpu.CompilerParams(collective_id=0, has_side_effects=True),
    )(tokens, key_codes, key_exponents.T, key_cotangent, inverse)


def solution(mesh):
    def body(tokens, key_codes, key_exponents, key_cotangent):
        row_count = tokens.shape[1] // (mesh.shape["node"] * mesh.shape["local"])
        run = fused if row_count % HEAD == 0 else on_device
        return run(tokens, key_codes, key_exponents, key_cotangent)

    return jax.shard_map(
        body,
        mesh=mesh,
        in_specs=(
            P(("node", "local"), None),
            P("local", None),
            P("local", None),
            P(("node", "local"), None),
        ),
        out_specs=(
            P(("node", "local"), None),
            P(("node", "local"), None),
            P(("node", "local"), None),
        ),
        check_vma=False,
    )
```

```python
import functools
import math

import jax
import jax.numpy as jnp
import numpy as np
from jax import lax
from jax.experimental import pallas as pl
from jax.experimental.pallas import tpu as pltpu
from jax.sharding import PartitionSpec as P

KVH = 4
HEAD = 128
QBLOCK = 256
SEQ = 8192
MESH = pl.DeviceIdType.MESH


THETA = 500000.0


def tables(positions):
    inverse = THETA ** (-(jnp.arange(HEAD // 2, dtype=jnp.float32) * 2.0 / HEAD))
    angles = positions.astype(jnp.float32)[:, None] * inverse[None, :]
    return (jnp.cos(angles), jnp.sin(angles))


def rotate(values, cosine, sine_part):
    count = values.shape[0]
    heads = values.reshape(count, KVH, HEAD)
    first_half = heads[:, :, : HEAD // 2]
    second_half = heads[:, :, HEAD // 2 :]
    cos_rows = cosine[:, None, :]
    sin_rows = sine_part[:, None, :]
    joined = jnp.concatenate(
        [
            first_half * cos_rows - second_half * sin_rows,
            second_half * cos_rows + first_half * sin_rows,
        ],
        axis=2,
    )
    return joined.reshape(count, KVH * HEAD)


def unrotate(values, cosine, sine_part):
    count = values.shape[0]
    heads = values.reshape(count, KVH, HEAD)
    first_half = heads[:, :, : HEAD // 2]
    second_half = heads[:, :, HEAD // 2 :]
    cos_rows = cosine[:, None, :]
    sin_rows = sine_part[:, None, :]
    joined = jnp.concatenate(
        [
            first_half * cos_rows + second_half * sin_rows,
            second_half * cos_rows - first_half * sin_rows,
        ],
        axis=2,
    )
    return joined.reshape(count, KVH * HEAD)


def quantize(partial_value):
    blocks = partial_value.reshape(partial_value.shape[0], partial_value.shape[1] // QBLOCK, QBLOCK)
    largest = jnp.max(jnp.abs(blocks), axis=2)
    block_scale = jnp.exp2(jnp.ceil(jnp.log2(largest + 1e-06)))
    code_values = (blocks / block_scale[:, :, None]).astype(jnp.bfloat16)
    return (code_values, block_scale.astype(jnp.bfloat16))


def expand_codes(code_values, block_scale):
    lead = code_values.shape[:-1]
    blocks = code_values.reshape(lead + (block_scale.shape[-1], QBLOCK))
    values = blocks.astype(jnp.float32) * block_scale.astype(jnp.float32)[..., None]
    return values.reshape(lead + (code_values.shape[-1],))


def on_device(tokens, key_codes, key_exponents, key_cotangent):
    node_count = lax.axis_size("node")
    local_count = lax.axis_size("local")
    tok_count = tokens.shape[0]
    width = tokens.shape[1]
    feature_count = key_codes.shape[1]
    expanded = jnp.repeat(jnp.exp2(key_exponents.astype(jnp.float32)), QBLOCK, axis=1)
    shard_weights = (key_codes.astype(jnp.float32) * expanded).astype(jnp.bfloat16)
    weights = lax.all_gather(shard_weights, "local", axis=0, tiled=True)
    device_index = lax.axis_index("node") * local_count + lax.axis_index("local")
    positions = (device_index * tok_count + jnp.arange(tok_count, dtype=jnp.int32)) % SEQ
    cosine, sine_part = tables(positions)
    pre_grad = unrotate(key_cotangent.astype(jnp.float32), cosine, sine_part).astype(jnp.bfloat16)
    partial_value = lax.dot_general(
        tokens, pre_grad, (((0,), (0,)), ((), ())), preferred_element_type=jnp.float32
    )
    code_values, block_scale = quantize(partial_value)
    row_count = width // (node_count * local_count)
    block_count = feature_count // QBLOCK
    code_grid = code_values.reshape(node_count, local_count, row_count, feature_count)
    scale_grid = block_scale.reshape(node_count, local_count, row_count, block_count)
    projected = jnp.dot(tokens, weights, preferred_element_type=jnp.float32)
    keys = rotate(projected, cosine, sine_part).astype(jnp.bfloat16)
    input_grad = lax.dot_general(
        pre_grad, weights, (((1,), (1,)), ((), ())), preferred_element_type=jnp.float32
    ).astype(jnp.bfloat16)
    got_codes, got_scales = (
        lax.all_to_all(code_grid, "local", split_axis=1, concat_axis=1, tiled=True),
        lax.all_to_all(scale_grid, "local", split_axis=1, concat_axis=1, tiled=True),
    )
    node_terms = jnp.sum(expand_codes(got_codes, got_scales), axis=1)
    summed = (
        lax.psum_scatter(node_terms.astype(jnp.bfloat16), "node", scatter_dimension=0, tiled=True)
        .astype(jnp.float32)
        .reshape(row_count, feature_count)
    )
    total_tokens = tok_count * node_count * local_count
    weight_grad = summed * (1.0 / math.sqrt(total_tokens))
    return (keys, input_grad, weight_grad)


def flip(index, distance):
    result = index
    bit = 1
    while bit <= distance:
        if distance & bit:
            result = result + bit - 2 * bit * lax.rem(lax.div(index, bit), 2)
        bit *= 2
    return result


def turn(values, cosine, signed_sine):
    parts = []
    for head in range(values.shape[1] // HEAD):
        piece = values[:, head * HEAD : (head + 1) * HEAD]
        parts.append(piece * cosine + pltpu.roll(piece, HEAD // 2, 1) * signed_sine)
    return jnp.concatenate(parts, axis=1)


def fused_kernel(
    nodes,
    locals_,
    chunks,
    tokens_hbm,
    codes_hbm,
    exponents_ref,
    cotangent_ref,
    inverse_ref,
    keys_ref,
    input_grad_ref,
    weight_grad_ref,
    tokens,
    codes,
    columns,
    pre,
    weights,
    outgoing,
    incoming,
    kept,
    load_sem,
    own_sem,
    column_send,
    column_recv,
    pre_send,
    pre_recv,
    weight_send,
    across_send,
    weight_recv,
    sum_send,
    sum_recv,
):
    node = lax.axis_index("node")
    local = lax.axis_index("local")
    count = tokens.shape[0]
    row_count = columns.shape[2]
    shard_rows = weights.shape[1]
    chunk_rows = shard_rows // chunks
    total = count * nodes * locals_

    barrier = pltpu.get_barrier_semaphore()
    for d in range(1, locals_):
        pl.semaphore_signal(barrier, inc=1, device_id=(node, flip(local, d)), device_id_type=MESH)
    reached = [1] + list(range(2, nodes, 2))
    for e in reached:
        pl.semaphore_signal(barrier, inc=1, device_id=(flip(node, e), local), device_id_type=MESH)

    load_codes = pltpu.make_async_copy(codes_hbm, codes, load_sem.at[0])
    load_codes.start()
    load_tokens = pltpu.make_async_copy(tokens_hbm, tokens, load_sem.at[1])
    load_tokens.start()

    def owned(e, d):
        first = (flip(node, e) * locals_ + flip(local, d)) * row_count
        return pl.ds(pl.multiple_of(first, row_count), row_count)

    order = list(range(nodes - 1, -1, -1))
    own = {}
    for e in order:
        own[e] = pltpu.make_async_copy(
            tokens_hbm.at[:, owned(e, 0)], columns.at[e, pl.ds(0, count), :], own_sem.at[e]
        )
        own[e].start()

    start = lax.rem((node * locals_ + local) * count, SEQ)
    positions = lax.rem(start + lax.broadcasted_iota(jnp.int32, (count, HEAD), 0), SEQ)
    angles = positions.astype(jnp.float32) * inverse_ref[...]
    cosine = jnp.cos(angles)
    sine = jnp.sin(angles)
    lane = lax.broadcasted_iota(jnp.int32, (count, HEAD), 1)
    signed_sine = jnp.where(lane < HEAD // 2, -sine, sine)
    pre[pl.ds(0, count), :] = turn(
        cotangent_ref[...].astype(jnp.float32), cosine, -signed_sine
    ).astype(jnp.bfloat16)

    pl.semaphore_wait(barrier, locals_ - 1 + len(reached))

    sends = []

    def send_pre(source, slot, distance):
        copy = pltpu.make_async_remote_copy(
            src_ref=pre.at[pl.ds(source * count, count), :],
            dst_ref=pre.at[pl.ds(slot * count, count), :],
            send_sem=pre_send.at[slot],
            recv_sem=pre_recv.at[slot],
            device_id=(node, flip(local, distance)),
            device_id_type=MESH,
        )
        copy.start()
        sends.append(copy)
        return copy

    pre_copies = {d: send_pre(0, d, d) for d in range(2, locals_, 2)}
    pre_copies[1] = send_pre(0, 1, 1)
    column_copies = {}
    for e in order:
        for d in range(locals_ - 1, 0, -1):
            copy = pltpu.make_async_remote_copy(
                src_ref=tokens_hbm.at[:, owned(e, d)],
                dst_ref=columns.at[e, pl.ds(d * count, count), :],
                send_sem=column_send.at[e, d],
                recv_sem=column_recv.at[e, d],
                device_id=(node, flip(local, d)),
                device_id_type=MESH,
            )
            copy.start()
            column_copies[e, d] = copy
            sends.append(copy)

    halves = [lax.rem(node, 2), lax.rem(lax.div(node, 2), 2)]

    def rows_of(turn_at, via):
        half = halves[turn_at % 2]
        part = turn_at * 2 + (1 - half if via else half)
        return pl.ds(pl.multiple_of(part * chunk_rows, chunk_rows), chunk_rows)

    def send_weights(source, slot, turn_at, via, device, kind, landing):
        copy = pltpu.make_async_remote_copy(
            src_ref=weights.at[source, rows_of(turn_at, via), :],
            dst_ref=weights.at[slot, rows_of(turn_at, via), :],
            send_sem=kind.at[slot, turn_at, via],
            recv_sem=weight_recv.at[slot, turn_at, landing],
            device_id=device,
            device_id_type=MESH,
        )
        copy.start()
        sends.append(copy)
        return copy

    partner = (node, flip(local, 1))
    across = [(flip(node, 1), local), (flip(node, 2), local)]
    turns = chunks // 2
    load_codes.wait()
    scale = jnp.left_shift(1, exponents_ref[...] + 15).astype(jnp.float32) * (2.0**-15)
    scale = jnp.transpose(jnp.concatenate([scale] * (8 // scale.shape[0]), axis=0))
    for block in range(codes.shape[1] // QBLOCK):
        lanes = pl.ds(block * QBLOCK, QBLOCK)
        weights[0, :, lanes] = (
            codes[:, lanes].astype(jnp.float32) * scale[:, block : block + 1]
        ).astype(jnp.bfloat16)
    arrivals = {}
    for turn_at in range(turns):
        for d in range(2, locals_, 2):
            device = (node, flip(local, d))
            arrivals[d, turn_at, 0] = send_weights(0, d, turn_at, 0, device, weight_send, 0)
        for via in range(2):
            arrivals[1, turn_at, via] = send_weights(0, 1, turn_at, via, partner, weight_send, via)

    for d in range(2, locals_, 2):
        pre_copies[d].wait_recv()
        pre_copies[d + 1] = send_pre(d, d + 1, 1)
    pre_copies[1].wait_recv()
    for d in range(3, locals_, 2):
        pre_copies[d].wait_recv()
    load_tokens.wait()
    projected = jnp.zeros((count, weights.shape[2]), jnp.float32)

    def use(slot, turn_at, via, projected):
        rows = rows_of(turn_at, via)
        first = flip(local, slot) * shard_rows + rows.start
        lanes = pl.ds(pl.multiple_of(first, chunk_rows), chunk_rows)
        block = weights[slot, rows, :]
        input_grad_ref[:, lanes] = lax.dot_general(
            pre[pl.ds(0, count), :],
            block,
            (((1,), (1,)), ((), ())),
            preferred_element_type=jnp.float32,
        ).astype(jnp.bfloat16)
        return projected + jnp.dot(tokens[:, lanes], block, preferred_element_type=jnp.float32)

    def late(turn_at, projected):
        for d in range(2, locals_, 2):
            arrivals[d, turn_at, 1].wait_recv()
            arrivals[d + 1, turn_at, 1] = send_weights(
                d, d + 1, turn_at, 1, partner, weight_send, 1
            )
            projected = use(d, turn_at, 1, projected)
        for d in range(3, locals_, 2):
            arrivals[d, turn_at, 1].wait_recv()
            projected = use(d, turn_at, 1, projected)
        return projected

    early = [(0, t, v) for t in range(turns) for v in range(2)]
    early += [(1, t, v) for t in range(turns) for v in range(2)]
    sum_copies = {}

    def send_sum(e, value, device):
        outgoing[e] = value.astype(jnp.bfloat16)
        copy = pltpu.make_async_remote_copy(
            src_ref=outgoing.at[e],
            dst_ref=incoming.at[e],
            send_sem=sum_send.at[e],
            recv_sem=sum_recv.at[e],
            device_id=device,
            device_id_type=MESH,
        )
        copy.start()
        sends.append(copy)
        return copy

    def finish(pair):
        sum_copies[2 * pair + 1].wait_recv()
        value = kept[pair] + incoming[2 * pair + 1].astype(jnp.float32)
        if pair:
            sum_copies[2 * pair] = send_sum(2 * pair, value, (flip(node, 2 * pair), local))
        else:
            kept[0] = value

    for e in order:
        own[e].wait()
        for d in range(1, locals_):
            column_copies[e, d].wait_recv()
        piece = lax.dot_general(
            columns[e], pre[...], (((0,), (0,)), ((), ())), preferred_element_type=jnp.float32
        )
        if e % 2 == 1:
            sum_copies[e] = send_sum(e, piece, (flip(node, 1), local))
        else:
            kept[e // 2] = piece
            if e + 2 < nodes:
                finish(e // 2 + 1)
        for _ in range(min(2, len(early))):
            slot, turn_at, via = early.pop(0)
            if slot == 1:
                arrivals[1, turn_at, via].wait_recv()
            projected = use(slot, turn_at, via, projected)

    for slot, turn_at, via in early:
        if slot == 1:
            arrivals[1, turn_at, via].wait_recv()
        projected = use(slot, turn_at, via, projected)
    for turn_at in range(turns):
        for d in range(2, locals_, 2):
            arrivals[d, turn_at, 0].wait_recv()
            arrivals[d, turn_at, 1] = send_weights(
                d, d, turn_at, 0, across[turn_at % 2], across_send, 1
            )
            arrivals[d + 1, turn_at, 0] = send_weights(
                d, d + 1, turn_at, 0, partner, weight_send, 0
            )
            projected = use(d, turn_at, 0, projected)
        for d in range(3, locals_, 2):
            arrivals[d, turn_at, 0].wait_recv()
            projected = use(d, turn_at, 0, projected)
        if turn_at == 0:
            finish(0)
        else:
            projected = late(turn_at - 1, projected)
    projected = late(turns - 1, projected)
    keys_ref[...] = turn(projected, cosine, signed_sine).astype(jnp.bfloat16)

    summed = kept[0]
    for e in range(nodes - 2, 0, -2):
        sum_copies[e].wait_recv()
        summed = summed + incoming[e].astype(jnp.float32)
    weight_grad_ref[...] = summed * (1.0 / math.sqrt(total))
    for copy in sends:
        copy.wait_send()


def fused(tokens, key_codes, key_exponents, key_cotangent):
    nodes = lax.axis_size("node")
    locals_ = lax.axis_size("local")
    count, width = tokens.shape
    features = key_codes.shape[1]
    shard_rows = key_codes.shape[0]
    row_count = width // (nodes * locals_)
    chunks = 8
    half = THETA ** (-(np.arange(HEAD // 2) * 2.0 / HEAD))
    inverse = jnp.asarray(np.concatenate([half, half])[None, :], jnp.float32)
    anywhere = pl.BlockSpec(memory_space=pl.ANY)
    vmem = pl.BlockSpec(memory_space=pltpu.VMEM)
    dma = pltpu.SemaphoreType.DMA
    return pl.pallas_call(
        functools.partial(fused_kernel, nodes, locals_, chunks),
        out_shape=(
            pltpu.VMEM((count, features), jnp.bfloat16),
            pltpu.VMEM((count, width), jnp.bfloat16),
            pltpu.VMEM((row_count, features), jnp.float32),
        ),
        in_specs=[anywhere, anywhere, vmem, vmem, vmem],
        out_specs=(vmem, vmem, vmem),
        scratch_shapes=[
            pltpu.VMEM((count, width), jnp.bfloat16),
            pltpu.VMEM((shard_rows, features), jnp.bfloat16),
            pltpu.VMEM((nodes, locals_ * count, row_count), jnp.bfloat16),
            pltpu.VMEM((locals_ * count, features), jnp.bfloat16),
            pltpu.VMEM((locals_, shard_rows, features), jnp.bfloat16),
            pltpu.VMEM((nodes, row_count, features), jnp.bfloat16),
            pltpu.VMEM((nodes, row_count, features), jnp.bfloat16),
            pltpu.VMEM((nodes // 2, row_count, features), jnp.float32),
            dma((2,)),
            dma((nodes,)),
            dma((nodes, locals_)),
            dma((nodes, locals_)),
            dma((locals_,)),
            dma((locals_,)),
            dma((locals_, chunks // 2, 2)),
            dma((locals_, chunks // 2, 2)),
            dma((locals_, chunks // 2, 2)),
            dma((nodes,)),
            dma((nodes,)),
        ],
        compiler_params=pltpu.CompilerParams(collective_id=0, has_side_effects=True),
    )(tokens, key_codes, key_exponents.T, key_cotangent, inverse)


def solution(mesh):
    def body(tokens, key_codes, key_exponents, key_cotangent):
        row_count = tokens.shape[1] // (mesh.shape["node"] * mesh.shape["local"])
        even = mesh.shape["node"] % 4 == 0 and mesh.shape["local"] % 2 == 0
        run = fused if even and row_count % HEAD == 0 else on_device
        return run(tokens, key_codes, key_exponents, key_cotangent)

    return jax.shard_map(
        body,
        mesh=mesh,
        in_specs=(
            P(("node", "local"), None),
            P("local", None),
            P("local", None),
            P(("node", "local"), None),
        ),
        out_specs=(
            P(("node", "local"), None),
            P(("node", "local"), None),
            P(("node", "local"), None),
        ),
        check_vma=False,
    )
```
